256 devices in a mesh: ctx: 16 (over x_lo, z), row: 16 (over y, x_hi, core).
Axes of the slice: x: 4 (x_hi: 2, x_lo: 2; x = x_hi * 2 + x_lo), y: 4, z: 8, core: 2. Of those that a mesh axis runs over, the one named last changes fastest.
Arguments:
- queries: bfloat16 [8192, 2048], P('ctx', 'row'), may hold values from -70 to 70
- keys: bfloat16 [8192, 2048], P('ctx', 'row'), may hold values from -4 to 4
- values: bfloat16 [8192, 2048], P('ctx', 'row'), may hold values from -24 to 24
- cross_queries: bfloat16 [8192, 2048], P('ctx', 'row'), may hold values from -70 to 70
- row_keys: bfloat16 [2048, 2048], P('ctx', 'row'), may hold values from -4 to 4
- row_values: bfloat16 [2048, 2048], P('ctx', 'row'), may hold values from -24 to 24
- incidence: int32 [8192, 4], P('ctx'), may hold values from 0 to 15, as said below
- out_weight: bfloat16 [2048, 2048], P('row'), may hold values from -0.125 to 0.125
- cotangent: bfloat16 [8192, 2048], P('ctx', 'row'), may hold values from -6 to 6
Outputs:
- mixed: bfloat16 [8192, 2048], P('ctx', 'row')
- grad_queries: float32 [8192, 2048], P('ctx', 'row')
- grad_keys: float32 [8192, 2048], P('ctx', 'row')
- grad_values: float32 [8192, 2048], P('ctx', 'row')
- grad_cross_queries: float32 [8192, 2048], P('ctx', 'row')
- grad_row_keys: float32 [2048, 2048], P('ctx', 'row')
- grad_row_values: float32 [2048, 2048], P('ctx', 'row')
- grad_weight: float32 [2048, 2048], P('row', 'ctx')
The draws below stay inside these ranges and needn't reach their ends.
Inputs may be any that keep to these rules, and one draw needn't show every extreme that they name: `incidence`: each token names 4 tiles of 128 constraint rows, repeats allowed, and attends exactly the rows of the tiles it names.
All inputs are finite; a program needn't handle non-finite values.
Results may differ from the reference program's by a relative error of at most 0.04.
Values may be sent and summed in bfloat16 or wider, within the bound.
A program may use at most 64 MiB of HBM per device.

```python
import math
import jax
import jax.numpy as jnp
from jax import lax

D = 2048
HEADS = 16
HEAD_DIM = 128
TILE = 128
NLIST = 4
SEQ = 8192
ROWS = 2048
NTILES = 16


def self_pair(key):
    query_key = jax.random.fold_in(key, 11)
    keys_key = jax.random.fold_in(key, 12)
    queries_raw = 2.0 * jax.random.truncated_normal(query_key, -3.0, 3.0, (SEQ, D), jnp.float32)
    keys_raw = jax.random.truncated_normal(keys_key, -4.0, 4.0, (SEQ, D), jnp.float32)
    return (queries_raw, keys_raw)


def cross_set(key):
    tile_first = (jax.random.permutation(jax.random.fold_in(key, 24), SEQ) % NTILES).astype(jnp.int32)
    tile_rest = jax.random.randint(jax.random.fold_in(key, 25), (SEQ, NLIST - 1), 0, NTILES, jnp.int32)
    lists = jnp.concatenate([tile_first[:, None], tile_rest], axis=1).astype(jnp.int32)
    query_key = jax.random.fold_in(key, 21)
    rowkey_key = jax.random.fold_in(key, 22)
    cross_raw = 2.0 * jax.random.truncated_normal(query_key, -3.0, 3.0, (SEQ, D), jnp.float32)
    rowkeys_raw = jax.random.truncated_normal(rowkey_key, -4.0, 4.0, (ROWS, D), jnp.float32)
    return (cross_raw, rowkeys_raw, lists)


def draw_queries(key, part):
    return self_pair(key)[0].astype(jnp.bfloat16)


def draw_keys(key, part):
    return self_pair(key)[1].astype(jnp.bfloat16)


def draw_cross_queries(key, part):
    return cross_set(key)[0].astype(jnp.bfloat16)


def draw_row_keys(key, part):
    return cross_set(key)[1].astype(jnp.bfloat16)


def draw_incidence(key, part):
    return cross_set(key)[2]


def steps_of(rng, shape, pieces, smallest, high):
    gain = 1.0
    for axis_at, parts in pieces:
        draws = jax.random.uniform(jax.random.fold_in(jax.random.fold_in(rng, 6), axis_at), (parts,), jnp.float32, smallest / len(pieces), high / len(pieces))
        gain = gain * jnp.repeat(jnp.exp(draws), shape[axis_at] // parts).reshape((-1,) + (1,) * (len(shape) - 1 - axis_at))
    return gain


def scatter_about(stream_key, dims, width, limit, cuts=(), kind=jnp.bfloat16):
    gain = steps_of(stream_key, dims, cuts, -0.22, 0.18) if cuts else 1.0
    drawn = jax.random.normal(stream_key, dims, jnp.float32) * width * gain
    return jnp.minimum(jnp.maximum(drawn, -limit), limit).astype(kind)


def setup_inputs(seed: int = 0) -> dict:
    seeds = jax.random.split(jax.random.key(seed), 10)
    queries = draw_queries(jax.random.fold_in(seeds[9], 71), 0)
    keys = draw_keys(jax.random.fold_in(seeds[9], 71), 0)
    values = scatter_about(seeds[2], (SEQ, D), 4.0, 24.0, ((0, 16), (1, 16)))
    cross_queries = draw_cross_queries(jax.random.fold_in(seeds[9], 71), 0)
    row_keys = draw_row_keys(jax.random.fold_in(seeds[9], 71), 0)
    row_values = scatter_about(seeds[5], (ROWS, D), 4.0, 24.0, ((0, 16), (1, 16)))
    incidence = draw_incidence(jax.random.fold_in(seeds[9], 71), 0)
    out_weight = scatter_about(seeds[7], (D, D), D ** -0.5, 0.125, ((0, 16),))
    cotangent = scatter_about(seeds[8], (SEQ, D), 1.0, 6.0, ((0, 16), (1, 16)))
    return {"queries": queries, "keys": keys, "values": values, "cross_queries": cross_queries, "row_keys": row_keys, "row_values": row_values, "incidence": incidence, "out_weight": out_weight, "cotangent": cotangent}


block_rows = 512

def to_bf16(array):
    return lax.optimization_barrier(array.astype(jnp.bfloat16))

def widen(array):
    return array.astype(jnp.float32)

def spread_heads(array):
    return array.reshape(array.shape[0], HEADS, HEAD_DIM).transpose(1, 0, 2)

def join_heads(array):
    return array.transpose(1, 0, 2).reshape(array.shape[1], HEADS * HEAD_DIM)

def log_totals(logits, allowed):
    masked = jnp.where(allowed, logits, -jnp.inf)
    highest = lax.optimization_barrier(jnp.max(masked, axis=-1, keepdims=True))
    return highest + jnp.log(lax.optimization_barrier(jnp.sum(jnp.exp(masked - highest), axis=-1, keepdims=True)))

def head_forward(queries_in, keys_in, values_in, allow_fn):
    rows_each = math.gcd(queries_in.shape[0], block_rows)
    block_count = queries_in.shape[0] // rows_each
    scaling = 1.0 / math.sqrt(HEAD_DIM)
    keys_wide = widen(keys_in)
    values_wide = widen(values_in)

    def one_block(element):
        block_index, queries_blk = element
        allowed = allow_fn(block_index * rows_each, rows_each)
        logits = scaling * jnp.dot(widen(queries_blk), keys_wide.T)
        log_sums = log_totals(logits, allowed)
        softmax = jnp.exp(jnp.where(allowed, logits - log_sums, -jnp.inf))
        outputs = jnp.dot(widen(to_bf16(softmax)), values_wide)
        return (outputs, log_sums[:, 0])
    stacked = queries_in.reshape(block_count, rows_each, HEAD_DIM)
    outputs, sums = lax.map(one_block, (jnp.arange(block_count, dtype=jnp.int32), stacked))
    return (outputs.reshape(-1, HEAD_DIM), sums.reshape(-1))

def head_backward(queries_in, keys_in, values_in, log_sums, outputs, grad_out, allow_fn):
    rows_each = math.gcd(queries_in.shape[0], block_rows)
    block_count = queries_in.shape[0] // rows_each
    scaling = 1.0 / math.sqrt(HEAD_DIM)
    keys_wide = widen(keys_in)
    values_wide = widen(values_in)
    deltas = lax.optimization_barrier(jnp.sum(widen(grad_out) * outputs, axis=-1))

    def one_block(state, element):
        block_index, queries_blk, grad_blk, sums_blk, delta_blk = element
        allowed = allow_fn(block_index * rows_each, rows_each)
        logits = scaling * jnp.dot(widen(queries_blk), keys_wide.T)
        softmax = jnp.exp(jnp.where(allowed, logits - sums_blk[:, None], -jnp.inf))
        grad_vals = state[1] + jnp.dot(widen(to_bf16(softmax)).T, widen(grad_blk))
        grad_probs = jnp.dot(widen(grad_blk), values_wide.T)
        grad_logits = widen(to_bf16(softmax * (grad_probs - delta_blk[:, None])))
        grad_keys = state[0] + scaling * jnp.dot(grad_logits.T, widen(queries_blk))
        grad_queries = scaling * jnp.dot(grad_logits, keys_wide)
        return ((grad_keys, grad_vals), grad_queries)
    zero_keys = jnp.zeros((keys_in.shape[0], HEAD_DIM), jnp.float32)
    items = (jnp.arange(block_count, dtype=jnp.int32), queries_in.reshape(block_count, rows_each, HEAD_DIM), grad_out.reshape(block_count, rows_each, HEAD_DIM), log_sums.reshape(block_count, rows_each), deltas.reshape(block_count, rows_each))
    (grad_keys, grad_vals), grad_queries = lax.scan(one_block, (zero_keys, zero_keys), items)
    return (grad_queries.reshape(-1, HEAD_DIM), grad_keys, grad_vals)

def reference(queries, keys, values, cross_queries, row_keys, row_values, incidence, out_weight, cotangent):

    def causal_allow(offset, length):
        positions = offset + jnp.arange(length, dtype=jnp.int32)
        return jnp.arange(SEQ, dtype=jnp.int32)[None, :] <= positions[:, None]

    def tile_allow(offset, length):
        lists = lax.dynamic_slice_in_dim(incidence, offset, length, 0)
        tiles = jnp.arange(ROWS, dtype=jnp.int32) // TILE
        return jnp.any(lists[:, :, None] == tiles[None, None, :], axis=1)

    def forward_one(element):
        query_h, key_h, value_h, cross_h, rowkey_h, rowvalue_h = element
        self_out, self_lse = head_forward(query_h, key_h, value_h, causal_allow)
        cross_out, cross_lse = head_forward(cross_h, rowkey_h, rowvalue_h, tile_allow)
        return (self_out, self_lse, cross_out, cross_lse)
    heads_in = (spread_heads(queries), spread_heads(keys), spread_heads(values), spread_heads(cross_queries), spread_heads(row_keys), spread_heads(row_values))
    self_out, self_lse, cross_out, cross_lse = lax.map(forward_one, heads_in)
    hidden = to_bf16(join_heads(self_out + cross_out))
    mixed = jnp.dot(hidden, out_weight, preferred_element_type=jnp.float32).astype(jnp.bfloat16)
    grad_weight = jnp.dot(hidden.T, cotangent, preferred_element_type=jnp.float32)
    grad_hidden = to_bf16(jnp.dot(cotangent, out_weight.T, preferred_element_type=jnp.float32))

    def backward_one(element):
        query_h, key_h, value_h, cross_h, rowkey_h, rowvalue_h, sums_s, outs_s, sums_c, outs_c, grad_h = element
        grad_q, grad_k, grad_v = head_backward(query_h, key_h, value_h, sums_s, outs_s, grad_h, causal_allow)
        grad_c, grad_rk, grad_rv = head_backward(cross_h, rowkey_h, rowvalue_h, sums_c, outs_c, grad_h, tile_allow)
        return (grad_q, grad_k, grad_v, grad_c, grad_rk, grad_rv)
    grads = lax.map(backward_one, heads_in + (self_lse, self_out, cross_lse, cross_out, spread_heads(grad_hidden)))
    grad_q, grad_k, grad_v, grad_c, grad_rk, grad_rv = grads
    return (mixed, join_heads(grad_q), join_heads(grad_k), join_heads(grad_v), join_heads(grad_c), join_heads(grad_rk), join_heads(grad_rv), grad_weight)
```

```python
import functools
import math

import jax
import jax.numpy as jnp
from jax import lax
from jax.experimental import pallas as pl
from jax.experimental.pallas import tpu as pltpu
from jax.sharding import PartitionSpec as P

MESH = pl.DeviceIdType.MESH
F32 = jnp.float32
BF16 = jnp.bfloat16
T = 512
HD = 128
TR = 128
NC = 16
NZ = 8
SCALE = 1.0 / math.sqrt(HD)
C2 = SCALE * math.log2(math.e)
LOG2E = math.log2(math.e)
NEG = -1e30

K0, RK0, V0, RV0, AG_HALF, AG_ALL = 0, 512, 640, 1152, 640, 1280
DK0, DRK0, GT0, DV0, DRV0, GB0, RS_HALF, RS_ALL = 0, 512, 640, 704, 1216, 1344, 704, 1408


def nn(a, b):
    return lax.dot_general(a, b, (((1,), (0,)), ((), ())), preferred_element_type=F32)


def nt(a, b):
    return lax.dot_general(a, b, (((1,), (1,)), ((), ())), preferred_element_type=F32)


def tn(a, b):
    return lax.dot_general(a, b, (((0,), (0,)), ((), ())), preferred_element_type=F32)


def body(
    q_ref, cq_ref, inc_ref, w_ref, k_hbm, v_hbm, rk_hbm, rv_hbm, cot_hbm,
    mixed_ref, gq_ref, gk_ref, gv_ref, gcq_ref, grk_ref, grv_ref, gw_ref,
    kv, cot, hid, wcol, snd, rcv, part, xsnd, xrcv, qt, cqt, dot_t, do_ref, ht,
    acc_s, acc_c, m_s, l_s, m_c, l_c, dl_s, dl_c, bias, dq_t, dcq_t,
    lsem, agx_s, agx_r, agz_s, agz_r, rsz_s, rsz_r, rsx_s, rsx_r, row_s, row_r, w_s, w_r,
):
    c = lax.axis_index("ctx")
    r = lax.axis_index("row")
    p, z = c // NZ, c % NZ
    y, xh, core = r // 4, (r // 2) % 2, r % 2

    def ctx_at(plane, depth):
        return {"ctx": plane * NZ + (depth + NZ) % NZ}

    def row_at(yy, xx, cc):
        return {"row": (((yy + 4) % 4) * 2 + xx) * 2 + cc}

    def plane_of(j):
        return p + j * (1 - 2 * p)

    def zmod(d):
        return (z + d + NZ) % NZ

    def remote(src, dst, ssem, rsem, device):
        return pltpu.make_async_remote_copy(
            src_ref=src, dst_ref=dst, send_sem=ssem, recv_sem=rsem, device_id=device, device_id_type=MESH
        )

    def agx():
        return remote(kv.at[p, z], kv.at[p, z], agx_s.at[0], agx_r.at[0], ctx_at(1 - p, z))

    def agx_in():
        return remote(kv.at[1 - p, z], kv.at[1 - p, z], agx_s.at[0], agx_r.at[0], ctx_at(1 - p, z))

    def agz(s, way, j, origin, half):
        ref = kv.at[plane_of(j), origin]
        if half:
            ref = ref.at[pl.ds(way * AG_HALF, AG_HALF)]
        return remote(ref, ref, agz_s.at[s - 1, way, j], agz_r.at[s - 1, way, j], ctx_at(p, z + 1 - 2 * way))

    def agz_out(s, way, j, half=False):
        return agz(s, way, j, zmod((2 * way - 1) * (s - 1)), half)

    def agz_in(s, way, j, half=False):
        return agz(s, way, j, zmod((2 * way - 1) * s), half)

    def rsz(s, way, j, half=False):
        src, dst = snd.at[s - 1, way, j], rcv.at[s - 1, way, j]
        if half:
            src = snd.at[0, 0, j].at[pl.ds(way * RS_HALF, RS_HALF)]
            dst = dst.at[pl.ds(way * RS_HALF, RS_HALF)]
        return remote(src, dst, rsz_s.at[s - 1, way, j], rsz_r.at[s - 1, way, j], ctx_at(p, z + 1 - 2 * way))

    def rsx():
        return remote(xsnd, xrcv, rsx_s.at[0], rsx_r.at[0], ctx_at(1 - p, z))

    def row_copy(buf, k, n, out):
        up, down, sib = row_at(y + 1, xh, core), row_at(y - 1, xh, core), row_at(y, xh, 1 - core)
        ym, yp, y2 = (y + 3) % 4, (y + 1) % 4, (y + 2) % 4
        mine, other = (core, core) if n < 5 else (core, 1 - core)
        if n == 0:
            ref = buf.at[y, core, xh if out else 1 - xh]
            dev = row_at(y, 1 - xh, core)
        elif n == 1:
            ref, dev = buf.at[y if out else ym, core], up
        elif n == 2:
            ref, dev = buf.at[y if out else yp, core], down
        elif n == 3:
            ref, dev = buf.at[ym if out else y2, core, :, pl.ds(0, T // 2)], up
        elif n == 4:
            ref, dev = buf.at[yp if out else y2, core, :, pl.ds(T // 2, T // 2)], down
        else:
            at = (y, ym, yp, y2)[n - 5]
            ref, dev = buf.at[at, mine if out else other], sib
        return remote(ref, ref, row_s.at[k, n], row_r.at[k, n], dev)

    def row_stage(buf, k, stage):
        waits, starts = {
            0: ((), (0,)), 1: ((0,), (1, 2, 5)), 2: ((1, 2), (3, 4, 6, 7)), 3: ((3, 4), (8,)), 4: ((5, 6, 7, 8), ()),
        }[stage]
        for n in waits:
            row_copy(buf, k, n, False).wait_recv()
        for n in starts:
            row_copy(buf, k, n, True).start()

    def w_out(j):
        to = (r + j) % NC
        return remote(
            w_ref.at[:, pl.ds(pl.multiple_of(to * HD, HD), HD)], wcol.at[r], w_s.at[j], w_r.at[j], {"row": to}
        )

    def w_in(j):
        at = (r + NC - j) % NC
        return remote(wcol.at[at], wcol.at[at], w_s.at[j], w_r.at[j], {"row": at})

    own = kv.at[p, z]
    loads = [
        pltpu.make_async_copy(k_hbm, own.at[pl.ds(K0, T)], lsem.at[0]),
        pltpu.make_async_copy(rk_hbm, own.at[pl.ds(RK0, TR)], lsem.at[1]),
        pltpu.make_async_copy(v_hbm, own.at[pl.ds(V0, T)], lsem.at[2]),
        pltpu.make_async_copy(rv_hbm, own.at[pl.ds(RV0, TR)], lsem.at[3]),
        pltpu.make_async_copy(cot_hbm, cot.at[y, core, xh], lsem.at[4]),
        pltpu.make_async_copy(w_ref.at[:, pl.ds(pl.multiple_of(r * HD, HD), HD)], wcol.at[r], lsem.at[5]),
    ]
    for load in loads:
        load.start()
    barrier = pltpu.get_barrier_semaphore()
    for device in (ctx_at(1 - p, z), ctx_at(p, z + 1), ctx_at(p, z - 1)):
        pl.semaphore_signal(barrier, inc=1, device_id=device, device_id_type=MESH)

    def greet(j, carry):
        pl.semaphore_signal(barrier, inc=1, device_id={"row": (r + j) % NC}, device_id_type=MESH)
        return carry

    lax.fori_loop(1, NC, greet, 0)
    for load in loads:
        load.wait()
    pl.semaphore_wait(barrier, NC + 2)

    agx().start()
    agz_out(1, 0, 0).start()
    agz_out(1, 1, 0).start()
    row_stage(cot, 0, 0)

    qt[...] = jnp.transpose(q_ref[...].astype(F32)).astype(BF16)
    cqt[...] = jnp.transpose(cq_ref[...].astype(F32)).astype(BF16)
    lanes = lax.broadcasted_iota(jnp.int32, (T, HD), 1)
    hit = jnp.zeros((T, HD), F32)
    for n in range(4):
        hit = jnp.where(inc_ref[:, n : n + 1] == lanes, 1.0, hit)
    bias[...] = (jnp.transpose(hit)[0:NC, :] - 1.0) * (-NEG)
    for ref in (acc_s, acc_c, l_s, l_c, dq_t, dcq_t):
        ref[...] = jnp.zeros_like(ref)
    for ref in (m_s, m_c):
        ref[...] = jnp.full_like(ref, NEG)
    for j in range(2):
        rcv[0, 0, j, RS_HALF:, :] = jnp.zeros((RS_ALL - RS_HALF, HD), BF16)
        rcv[0, 1, j, :RS_HALF, :] = jnp.zeros((RS_HALF, HD), BF16)

    def online(logits, values, m_ref, l_ref, acc_ref):
        m_old = m_ref[...]
        m_new = jnp.maximum(m_old, jnp.max(logits, axis=0, keepdims=True))
        probs = jnp.exp2(logits - m_new)
        fade = jnp.exp2(m_old - m_new)
        l_ref[...] = l_ref[...] * fade + jnp.sum(probs, axis=0, keepdims=True)
        acc_ref[...] = acc_ref[...] * fade + tn(values, probs.astype(BF16))
        m_ref[...] = m_new

    def causal(x, fill):
        keep = lax.broadcasted_iota(jnp.int32, (T, T), 0) <= lax.broadcasted_iota(jnp.int32, (T, T), 1)
        return jnp.where(keep, x, fill)

    def self_forward(pa, zb, diagonal):
        logits = nn(kv[pa, zb, pl.ds(K0, T), :], qt[...]) * C2
        if diagonal:
            logits = causal(logits, NEG)
        online(logits, kv[pa, zb, pl.ds(V0, T), :], m_s, l_s, acc_s)

    def cross_logits(pa, zb):
        return nn(kv[pa, zb, pl.ds(RK0, TR), :], cqt[...]) * C2 + bias[pl.ds(pa * NZ + zb, 1), :]

    def cross_forward(pa, zb):
        online(cross_logits(pa, zb), kv[pa, zb, pl.ds(RV0, TR), :], m_c, l_c, acc_c)

    self_forward(p, z, True)
    cross_forward(p, z)

    def forward_step(t, carry):
        v = t - 2
        s = jnp.where(t < 2, 0, v // 4 + 1)
        i = jnp.where(t < 2, 1, v % 4)
        way, j = i // 2, i % 2

        @pl.when(t == 1)
        def _():
            agx_in().wait_recv()
            agz_out(1, 0, 1).start()
            agz_out(1, 1, 1).start()
            row_stage(cot, 0, 1)

        for hop in range(1, 5):

            @pl.when(v == 4 * (hop - 1))
            def _():
                for jj in range(2):
                    for ww in range(2):
                        agz_in(hop, ww, jj, hop == 4).wait_recv()
                        if hop < 4:
                            agz_out(hop + 1, ww, jj, hop == 3).start()
                if hop == 1:
                    for jj in range(1, NC):
                        w_out(jj).start()
                if hop > 1:
                    row_stage(cot, 0, hop)

        pa = plane_of(j)
        zb = zmod((2 * way - 1) * s)

        @pl.when(pa * NZ + zb < c)
        def _():
            self_forward(pa, zb, False)

        cross_forward(pa, zb)
        return carry

    lax.fori_loop(1, NC, forward_step, 0)

    grad = jnp.zeros((T, HD), F32)
    for n in range(NC):
        grad = grad + nt(cot[n // 4, n % 2, (n // 2) % 2], w_ref[:, n * HD : (n + 1) * HD])
    grad = grad.astype(BF16)
    do_ref[...] = grad
    grad_t = jnp.transpose(grad.astype(F32))
    dot_t[...] = grad_t.astype(BF16)
    out_s = acc_s[...] / l_s[...]
    out_c = acc_c[...] / l_c[...]
    hidden_t = out_s + out_c
    ht[...] = hidden_t.astype(BF16)
    hid[y, core, xh] = jnp.transpose(hidden_t).astype(BF16)
    dl_s[...] = jnp.sum(grad_t * out_s, axis=0, keepdims=True)
    dl_c[...] = jnp.sum(grad_t * out_c, axis=0, keepdims=True)
    m_s[...] = m_s[...] + jnp.log(l_s[...]) * LOG2E
    m_c[...] = m_c[...] + jnp.log(l_c[...]) * LOG2E
    row_stage(hid, 1, 0)

    def logit_grads(logits, lse_ref, delta_ref, values, diagonal):
        probs = jnp.exp2(logits - lse_ref[...])
        if diagonal:
            probs = causal(probs, 0.0)
        dlogits = probs * (nn(values, dot_t[...]) - delta_ref[...])
        return probs.astype(BF16), dlogits.astype(BF16)

    def self_backward(pa, zb, slot, diagonal):
        keys, values = kv[pa, zb, pl.ds(K0, T), :], kv[pa, zb, pl.ds(V0, T), :]
        probs, dlogits = logit_grads(nn(keys, qt[...]) * C2, m_s, dl_s, values, diagonal)
        part[slot, pl.ds(DV0, T), :] = nn(probs, do_ref[...])
        part[slot, pl.ds(DK0, T), :] = nn(dlogits, q_ref[...])
        dq_t[...] += tn(keys, dlogits)

    def cross_backward(pa, zb, slot):
        probs, dlogits = logit_grads(cross_logits(pa, zb), m_c, dl_c, kv[pa, zb, pl.ds(RV0, TR), :], False)
        part[slot, pl.ds(DRV0, TR), :] = nn(probs, do_ref[...])
        part[slot, pl.ds(DRK0, TR), :] = nn(dlogits, cq_ref[...])
        dcq_t[...] += tn(kv[pa, zb, pl.ds(RK0, TR), :], dlogits)
        b = pa * NZ + zb
        weight = nn(ht[...], cot[b // 4, b % 2, (b // 2) % 2])
        part[slot, pl.ds(GT0, HD // 2), :] = weight[: HD // 2]
        part[slot, pl.ds(GB0, HD // 2), :] = weight[HD // 2 :]

    def backward_step(u, carry):
        v = u - 2
        first, last = u < 2, u == 14
        s = jnp.where(first, 1, v // 4 + 2)
        i = jnp.where(first, u, jnp.where(last, 1, v % 4))
        way, j = i // 2, i % 2
        slot = jnp.where(first, u, v % 4)
        d = 5 - s
        pa = plane_of(j)
        zb = zmod((1 - 2 * way) * d)

        @pl.when(pa * NZ + zb < c)
        def _():
            self_backward(pa, zb, slot, False)

        @pl.when(pa * NZ + zb > c)
        def _():
            part[slot, pl.ds(DK0, T), :] = jnp.zeros((T, HD), F32)
            part[slot, pl.ds(DV0, T), :] = jnp.zeros((T, HD), F32)

        cross_backward(pa, zb, slot)

        @pl.when(u == 1)
        def _():
            for jj in range(2):
                snd[0, 0, jj] = part[jj].astype(BF16)
                rsz(1, 0, jj, True).start()
                rsz(1, 1, jj, True).start()
            row_stage(hid, 1, 1)

        for hop in range(2, 5):

            @pl.when(v == 4 * (hop - 2) + 3)
            def _():
                def pass_on(n, inner):
                    ww, jj = n // 2, n % 2
                    rsz(hop - 1, ww, jj, hop == 2).wait_recv()
                    snd[hop - 1, ww, jj] = (part[n] + rcv[hop - 2, ww, jj].astype(F32)).astype(BF16)
                    rsz(hop, ww, jj).start()
                    return inner

                lax.fori_loop(0, 4, pass_on, 0)
                row_stage(hid, 1, hop)

        return carry

    lax.fori_loop(0, NC - 1, backward_step, 0)
    self_backward(p, z, 1, True)
    cross_backward(p, z, 1)

    for j in range(1, NC):
        w_in(j).wait_recv()
    mix = jnp.zeros((T, HD), F32)
    for n in range(NC):
        mix = mix + nn(hid[n // 4, n % 2, (n // 2) % 2], wcol[n])
    mixed_ref[...] = mix.astype(BF16)
    gq_ref[...] = jnp.transpose(dq_t[...]) * SCALE
    gcq_ref[...] = jnp.transpose(dcq_t[...]) * SCALE

    rsz(4, 0, 1).wait_recv()
    rsz(4, 1, 1).wait_recv()
    xsnd[...] = (part[0] + rcv[3, 0, 1].astype(F32) + rcv[3, 1, 1].astype(F32)).astype(BF16)
    rsx().start()
    rsz(4, 0, 0).wait_recv()
    rsz(4, 1, 0).wait_recv()
    part[1] = part[1] + rcv[3, 0, 0].astype(F32) + rcv[3, 1, 0].astype(F32)
    rsx().wait_recv()

    def total(at, rows):
        return part[1, pl.ds(at, rows), :] + xrcv[pl.ds(at, rows), :].astype(F32)

    gk_ref[...] = total(DK0, T) * SCALE
    gv_ref[...] = total(DV0, T)
    grk_ref[...] = total(DRK0, TR) * SCALE
    grv_ref[...] = total(DRV0, TR)
    gw_ref[pl.ds(0, HD // 2), :] = total(GT0, HD // 2)
    gw_ref[pl.ds(HD // 2, HD // 2), :] = total(GB0, HD // 2)

    agx().wait_send()
    rsx().wait_send()
    for jj in range(2):
        for ww in range(2):
            for s in range(1, 5):
                agz_out(s, ww, jj, s == 4).wait_send()
                rsz(s, ww, jj, s == 1).wait_send()
    for n in range(9):
        row_copy(cot, 0, n, True).wait_send()
        row_copy(hid, 1, n, True).wait_send()
    for j in range(1, NC):
        w_out(j).wait_send()


def shards(queries, keys, values, cross_queries, row_keys, row_values, incidence, out_weight, cotangent):
    vmem = pl.BlockSpec(memory_space=pltpu.VMEM)
    hbm = pl.BlockSpec(memory_space=pl.ANY)
    dma = pltpu.SemaphoreType.DMA
    big, small = jax.ShapeDtypeStruct((T, HD), F32), jax.ShapeDtypeStruct((TR, HD), F32)
    wide = pltpu.VMEM((HD, T), F32)
    line = pltpu.VMEM((1, T), F32)
    return pl.pallas_call(
        body,
        out_shape=(jax.ShapeDtypeStruct((T, HD), BF16), big, big, big, big, small, small, small),
        in_specs=[vmem] * 4 + [hbm] * 5,
        out_specs=[vmem] * 8,
        scratch_shapes=[
            pltpu.VMEM((2, NZ, AG_ALL, HD), BF16),
            pltpu.VMEM((4, 2, 2, T, HD), BF16),
            pltpu.VMEM((4, 2, 2, T, HD), BF16),
            pltpu.VMEM((NC, HD, HD), BF16),
            pltpu.VMEM((4, 2, 2, RS_ALL, HD), BF16),
            pltpu.VMEM((4, 2, 2, RS_ALL, HD), BF16),
            pltpu.VMEM((4, RS_ALL, HD), F32),
            pltpu.VMEM((RS_ALL, HD), BF16),
            pltpu.VMEM((RS_ALL, HD), BF16),
            pltpu.VMEM((HD, T), BF16),
            pltpu.VMEM((HD, T), BF16),
            pltpu.VMEM((HD, T), BF16),
            pltpu.VMEM((T, HD), BF16),
            pltpu.VMEM((HD, T), BF16),
            wide, wide, line, line, line, line, line, line,
            pltpu.VMEM((NC, T), F32),
            wide, wide,
            dma((6,)), dma((1,)), dma((1,)), dma((4, 2, 2)), dma((4, 2, 2)), dma((4, 2, 2)), dma((4, 2, 2)),
            dma((1,)), dma((1,)), dma((2, 9)), dma((2, 9)), dma((NC,)), dma((NC,)),
        ],
        compiler_params=pltpu.CompilerParams(
            collective_id=0, has_side_effects=True, vmem_limit_bytes=60 * 1024 * 1024
        ),
        name="attention_layer",
    )(queries, cross_queries, incidence, out_weight, keys, values, row_keys, row_values, cotangent)


def solution(mesh):
    both = P("ctx", "row")
    return jax.shard_map(
        shards,
        mesh=mesh,
        in_specs=(both, both, both, both, both, both, P("ctx", None), P("row", None), both),
        out_specs=(both, both, both, both, both, both, both, P("row", "ctx")),
        check_vma=False,
    )
```

```python
import functools
import math

import jax
import jax.numpy as jnp
from jax import lax
from jax.experimental import pallas as pl
from jax.experimental.pallas import tpu as pltpu
from jax.sharding import PartitionSpec as P

MESH = pl.DeviceIdType.MESH
F32 = jnp.float32
BF16 = jnp.bfloat16
T = 512
HD = 128
TR = 128
NC = 16
NZ = 8
SCALE = 1.0 / math.sqrt(HD)
C2 = SCALE * math.log2(math.e)
LOG2E = math.log2(math.e)
NEG = -1e30

K0, RK0, RV0, V0, AG_HALF, AG_ALL = 0, 512, 640, 768, 640, 1280
AG_MID, AG_MID_N = 512, 256
DK0, DRK0, GT0, GB0, DRV0, DV0, RS_HALF, RS_ALL = 0, 512, 640, 704, 768, 896, 704, 1408
RS_MID, RS_MID_N = 512, 384


def nn(a, b):
    return lax.dot_general(a, b, (((1,), (0,)), ((), ())), preferred_element_type=F32)


def nt(a, b):
    return lax.dot_general(a, b, (((1,), (1,)), ((), ())), preferred_element_type=F32)


def tn(a, b):
    return lax.dot_general(a, b, (((0,), (0,)), ((), ())), preferred_element_type=F32)


def body(
    q_ref, cq_ref, inc_ref, w_ref, k_hbm, v_hbm, rk_hbm, rv_hbm, cot_hbm,
    mixed_ref, gq_ref, gk_ref, gv_ref, gcq_ref, grk_ref, grv_ref, gw_ref,
    kv, cot, hid, wcol, snd, rcv, part, xsnd, xrcv, qt, cqt, dot_t, do_ref, ht,
    acc_s, acc_c, m_s, l_s, m_c, l_c, dl_s, dl_c, bias, dq_t, dcq_t, xr,
    lsem, agx_s, agx_r, agz_s, agz_r, rsz_s, rsz_r, rsx_s, rsx_r, row_s, row_r, w_s, w_r,
    rel_s, rel_r, shr_s, shr_r,
):
    c = lax.axis_index("ctx")
    r = lax.axis_index("row")
    p, z = c // NZ, c % NZ
    y, xh, core = r // 4, (r // 2) % 2, r % 2

    def ctx_at(plane, depth):
        return {"ctx": plane * NZ + (depth + NZ) % NZ}

    def row_at(yy, xx, cc):
        return {"row": (((yy + 4) % 4) * 2 + xx) * 2 + cc}

    def plane_of(j):
        return p + j * (1 - 2 * p)

    def zmod(d):
        return (z + d + NZ) % NZ

    def remote(src, dst, ssem, rsem, device):
        return pltpu.make_async_remote_copy(
            src_ref=src, dst_ref=dst, send_sem=ssem, recv_sem=rsem, device_id=device, device_id_type=MESH
        )

    def on_plane(plane, act):
        pl.when(p == plane)(act)

    def agx(out, plane):
        ref = kv.at[p if out else 1 - p, z]
        if (plane == 1) == out:
            ref = ref.at[pl.ds(AG_MID, AG_MID_N)]
        return remote(ref, ref, agx_s.at[0], agx_r.at[0], ctx_at(1 - p, z))

    def agz(s, way, j, out, middle):
        ref = kv.at[plane_of(j), zmod((2 * way - 1) * (s - 1 if out else s))]
        half = s == 4
        if middle:
            n = AG_MID_N // 2 if half else AG_MID_N
            ref = ref.at[pl.ds(AG_MID + (way * n if half else 0), n)]
        elif half:
            ref = ref.at[pl.ds(way * AG_HALF, AG_HALF)]
        return remote(ref, ref, agz_s.at[s - 1, way, j], agz_r.at[s - 1, way, j], ctx_at(p, z + 1 - 2 * way))

    def relay(s, way):
        ref = kv.at[0, zmod((2 * way - 1) * s)]
        if s == 4:
            ref = ref.at[pl.ds(way * AG_HALF, AG_HALF)]
        n = 2 * (s - 3) + way
        return remote(ref, ref, rel_s.at[n], rel_r.at[n], ctx_at(1 - p, z))

    def agz_start(s, way, j):
        if j == 0:
            agz(s, way, 0, True, False).start()
            return
        on_plane(0, lambda: agz(s, way, 1, True, True).start())
        if s < 3:
            on_plane(1, lambda: agz(s, way, 1, True, False).start())

    def agz_wait(s, way, j):
        if j == 0:
            agz(s, way, 0, False, False).wait_recv()
            if s >= 3:
                on_plane(0, lambda: relay(s, way).start())
            return
        on_plane(0, lambda: agz(s, way, 1, False, True).wait_recv())
        on_plane(1, lambda: (agz(s, way, 1, False, False) if s < 3 else relay(s, way)).wait_recv())

    def agz_sent(s, way, j):
        if j == 0:
            agz(s, way, 0, True, False).wait_send()
            if s >= 3:
                on_plane(0, lambda: relay(s, way).wait_send())
            return
        on_plane(0, lambda: agz(s, way, 1, True, True).wait_send())
        if s < 3:
            on_plane(1, lambda: agz(s, way, 1, True, False).wait_send())

    def rsz(s, way, j, middle):
        half = s == 1
        src = snd.at[0, 0, j] if half else snd.at[s - 1, way, j]
        dst = rcv.at[s - 1, way, j]
        if middle:
            n = RS_MID_N // 2 if half else RS_MID_N
            rows = pl.ds(RS_MID + (way * n if half else 0), n)
            src, dst = src.at[rows], dst.at[rows]
        elif half:
            rows = pl.ds(way * RS_HALF, RS_HALF)
            src, dst = src.at[rows], dst.at[rows]
        return remote(src, dst, rsz_s.at[s - 1, way, j], rsz_r.at[s - 1, way, j], ctx_at(p, z + 1 - 2 * way))

    def share(n):
        src = snd.at[0, 0, 1] if isinstance(n, int) and n == 0 else snd.at[1, n - 1, 1]
        return remote(src, xr.at[n], shr_s.at[n], shr_r.at[n], ctx_at(1 - p, z))

    def rsz_start(s, way, j):
        if j == 0:
            rsz(s, way, 0, False).start()
            return
        on_plane(0, lambda: rsz(s, way, 1, True).start())
        if s >= 3:
            on_plane(1, lambda: rsz(s, way, 1, False).start())
        elif s == 2:
            on_plane(1, lambda: share(1 + way).start())

    def rsz_wait(s, way, j):
        if j == 0:
            rsz(s, way, 0, False).wait_recv()
            return
        on_plane(0, lambda: rsz(s, way, 1, True).wait_recv())
        if s >= 3:
            on_plane(1, lambda: rsz(s, way, 1, False).wait_recv())

    def rsz_sent(s, way, j):
        if j == 0:
            rsz(s, way, 0, False).wait_send()
            return
        on_plane(0, lambda: rsz(s, way, 1, True).wait_send())
        if s >= 3:
            on_plane(1, lambda: rsz(s, way, 1, False).wait_send())

    def rsx(middle):
        rows = pl.ds(RS_MID, RS_MID_N) if middle else pl.ds(0, RS_ALL)
        return remote(xsnd.at[rows], xrcv.at[rows], rsx_s.at[0], rsx_r.at[0], ctx_at(1 - p, z))

    def row_copy(buf, k, n, out):
        up, down, sib = row_at(y + 1, xh, core), row_at(y - 1, xh, core), row_at(y, xh, 1 - core)
        ym, yp, y2 = (y + 3) % 4, (y + 1) % 4, (y + 2) % 4
        mine, other = (core, core) if n < 5 else (core, 1 - core)
        if n == 0:
            ref = buf.at[y, core, xh if out else 1 - xh]
            dev = row_at(y, 1 - xh, core)
        elif n == 1:
            ref, dev = buf.at[y if out else ym, core], up
        elif n == 2:
            ref, dev = buf.at[y if out else yp, core], down
        elif n == 3:
            ref, dev = buf.at[ym if out else y2, core, :, pl.ds(0, T // 2)], up
        elif n == 4:
            ref, dev = buf.at[yp if out else y2, core, :, pl.ds(T // 2, T // 2)], down
        else:
            at = (y, ym, yp, y2)[n - 5]
            ref, dev = buf.at[at, mine if out else other], sib
        return remote(ref, ref, row_s.at[k, n], row_r.at[k, n], dev)

    def row_stage(buf, k, stage):
        waits, starts = {
            0: ((), (0,)), 1: ((0,), (1, 2, 5)), 2: ((1, 2), (3, 4, 6, 7)), 3: ((3, 4), (8,)), 4: ((5, 6, 7, 8), ()),
        }[stage]
        for n in waits:
            row_copy(buf, k, n, False).wait_recv()
        for n in starts:
            row_copy(buf, k, n, True).start()

    def w_out(j):
        to = (r + j) % NC
        return remote(
            w_ref.at[:, pl.ds(pl.multiple_of(to * HD, HD), HD)], wcol.at[r], w_s.at[j], w_r.at[j], {"row": to}
        )

    def w_in(j):
        at = (r + NC - j) % NC
        return remote(wcol.at[at], wcol.at[at], w_s.at[j], w_r.at[j], {"row": at})

    own = kv.at[p, z]
    loads = [
        pltpu.make_async_copy(k_hbm, own.at[pl.ds(K0, T)], lsem.at[0]),
        pltpu.make_async_copy(rk_hbm, own.at[pl.ds(RK0, TR)], lsem.at[1]),
        pltpu.make_async_copy(v_hbm, own.at[pl.ds(V0, T)], lsem.at[2]),
        pltpu.make_async_copy(rv_hbm, own.at[pl.ds(RV0, TR)], lsem.at[3]),
        pltpu.make_async_copy(cot_hbm, cot.at[y, core, xh], lsem.at[4]),
        pltpu.make_async_copy(w_ref.at[:, pl.ds(pl.multiple_of(r * HD, HD), HD)], wcol.at[r], lsem.at[5]),
    ]
    for load in loads:
        load.start()
    barrier = pltpu.get_barrier_semaphore()
    for device in (ctx_at(1 - p, z), ctx_at(p, z + 1), ctx_at(p, z - 1)):
        pl.semaphore_signal(barrier, inc=1, device_id=device, device_id_type=MESH)

    def greet(j, carry):
        pl.semaphore_signal(barrier, inc=1, device_id={"row": (r + j) % NC}, device_id_type=MESH)
        return carry

    lax.fori_loop(1, NC, greet, 0)
    for load in loads:
        load.wait()
    pl.semaphore_wait(barrier, NC + 2)

    for plane in range(2):
        on_plane(plane, lambda: agx(True, plane).start())
    agz_start(1, 0, 0)
    agz_start(1, 1, 0)
    row_stage(cot, 0, 0)

    qt[...] = jnp.transpose(q_ref[...].astype(F32)).astype(BF16)
    cqt[...] = jnp.transpose(cq_ref[...].astype(F32)).astype(BF16)
    lanes = lax.broadcasted_iota(jnp.int32, (T, HD), 1)
    hit = jnp.zeros((T, HD), F32)
    for n in range(4):
        hit = jnp.where(inc_ref[:, n : n + 1] == lanes, 1.0, hit)
    bias[...] = (jnp.transpose(hit)[0:NC, :] - 1.0) * (-NEG)
    for ref in (acc_s, acc_c, l_s, l_c, dq_t, dcq_t):
        ref[...] = jnp.zeros_like(ref)
    for ref in (m_s, m_c):
        ref[...] = jnp.full_like(ref, NEG)
    for j in range(2):
        rcv[0, 0, j, RS_HALF:, :] = jnp.zeros((RS_ALL - RS_HALF, HD), BF16)
        rcv[0, 1, j, :RS_HALF, :] = jnp.zeros((RS_HALF, HD), BF16)

    @pl.when(p == 1)
    def _():
        for way in range(2):
            rcv[0, way, 1] = jnp.zeros((RS_ALL, HD), BF16)
            rcv[1, way, 1] = jnp.zeros((RS_ALL, HD), BF16)
        xr[...] = jnp.zeros_like(xr)
        xrcv[...] = jnp.zeros_like(xrcv)

    def online(logits, values, m_ref, l_ref, acc_ref):
        m_old = m_ref[...]
        m_new = jnp.maximum(m_old, jnp.max(logits, axis=0, keepdims=True))
        probs = jnp.exp2(logits - m_new)
        fade = jnp.exp2(m_old - m_new)
        l_ref[...] = l_ref[...] * fade + jnp.sum(probs, axis=0, keepdims=True)
        acc_ref[...] = acc_ref[...] * fade + tn(values, probs.astype(BF16))
        m_ref[...] = m_new

    def causal(x, fill):
        keep = lax.broadcasted_iota(jnp.int32, (T, T), 0) <= lax.broadcasted_iota(jnp.int32, (T, T), 1)
        return jnp.where(keep, x, fill)

    def self_forward(pa, zb, diagonal):
        logits = nn(kv[pa, zb, pl.ds(K0, T), :], qt[...]) * C2
        if diagonal:
            logits = causal(logits, NEG)
        online(logits, kv[pa, zb, pl.ds(V0, T), :], m_s, l_s, acc_s)

    def cross_logits(pa, zb):
        return nn(kv[pa, zb, pl.ds(RK0, TR), :], cqt[...]) * C2 + bias[pl.ds(pa * NZ + zb, 1), :]

    def cross_forward(pa, zb):
        online(cross_logits(pa, zb), kv[pa, zb, pl.ds(RV0, TR), :], m_c, l_c, acc_c)

    self_forward(p, z, True)
    cross_forward(p, z)

    def forward_step(t, carry):
        v = t - 2
        s = jnp.where(t < 2, 0, v // 4 + 1)
        i = jnp.where(t < 2, 1, v % 4)
        way, j = i // 2, i % 2

        @pl.when(t == 1)
        def _():
            for plane in range(2):
                on_plane(plane, lambda: agx(False, plane).wait_recv())
            agz_start(1, 0, 1)
            agz_start(1, 1, 1)
            row_stage(cot, 0, 1)

        for hop in range(1, 5):

            @pl.when(v == 4 * (hop - 1))
            def _():
                for jj in range(2):
                    for ww in range(2):
                        agz_wait(hop, ww, jj)
                        if hop < 4:
                            agz_start(hop + 1, ww, jj)
                if hop == 1:
                    for jj in range(1, NC):
                        w_out(jj).start()
                if hop > 1:
                    row_stage(cot, 0, hop)

        pa = plane_of(j)
        zb = zmod((2 * way - 1) * s)

        @pl.when(pa * NZ + zb < c)
        def _():
            self_forward(pa, zb, False)

        cross_forward(pa, zb)
        return carry

    lax.fori_loop(1, NC, forward_step, 0)

    grad = jnp.zeros((T, HD), F32)
    for n in range(NC):
        grad = grad + nt(cot[n // 4, n % 2, (n // 2) % 2], w_ref[:, n * HD : (n + 1) * HD])
    grad = grad.astype(BF16)
    do_ref[...] = grad
    grad_t = jnp.transpose(grad.astype(F32))
    dot_t[...] = grad_t.astype(BF16)
    out_s = acc_s[...] / l_s[...]
    out_c = acc_c[...] / l_c[...]
    hidden_t = out_s + out_c
    ht[...] = hidden_t.astype(BF16)
    hid[y, core, xh] = jnp.transpose(hidden_t).astype(BF16)
    dl_s[...] = jnp.sum(grad_t * out_s, axis=0, keepdims=True)
    dl_c[...] = jnp.sum(grad_t * out_c, axis=0, keepdims=True)
    m_s[...] = m_s[...] + jnp.log(l_s[...]) * LOG2E
    m_c[...] = m_c[...] + jnp.log(l_c[...]) * LOG2E
    row_stage(hid, 1, 0)

    def logit_grads(logits, lse_ref, delta_ref, values, diagonal):
        probs = jnp.exp2(logits - lse_ref[...])
        if diagonal:
            probs = causal(probs, 0.0)
        dlogits = probs * (nn(values, dot_t[...]) - delta_ref[...])
        return probs.astype(BF16), dlogits.astype(BF16)

    def self_backward(pa, zb, slot, diagonal):
        keys, values = kv[pa, zb, pl.ds(K0, T), :], kv[pa, zb, pl.ds(V0, T), :]
        probs, dlogits = logit_grads(nn(keys, qt[...]) * C2, m_s, dl_s, values, diagonal)
        part[slot, pl.ds(DV0, T), :] = nn(probs, do_ref[...])
        part[slot, pl.ds(DK0, T), :] = nn(dlogits, q_ref[...])
        dq_t[...] += tn(keys, dlogits)

    def cross_backward(pa, zb, slot):
        probs, dlogits = logit_grads(cross_logits(pa, zb), m_c, dl_c, kv[pa, zb, pl.ds(RV0, TR), :], False)
        part[slot, pl.ds(DRV0, TR), :] = nn(probs, do_ref[...])
        part[slot, pl.ds(DRK0, TR), :] = nn(dlogits, cq_ref[...])
        dcq_t[...] += tn(kv[pa, zb, pl.ds(RK0, TR), :], dlogits)
        b = pa * NZ + zb
        weight = nn(ht[...], cot[b // 4, b % 2, (b // 2) % 2])
        part[slot, pl.ds(GT0, HD // 2), :] = weight[: HD // 2]
        part[slot, pl.ds(GB0, HD // 2), :] = weight[HD // 2 :]

    def backward_step(u, carry):
        v = u - 2
        first, last = u < 2, u == 14
        s = jnp.where(first, 1, v // 4 + 2)
        i = jnp.where(first, 1 - u, jnp.where(last, 1, v % 4))
        way, j = i // 2, i % 2
        slot = jnp.where(first, 1 - u, v % 4)
        d = 5 - s
        pa = plane_of(j)
        zb = zmod((1 - 2 * way) * d)

        @pl.when(pa * NZ + zb < c)
        def _():
            self_backward(pa, zb, slot, False)

        @pl.when(pa * NZ + zb > c)
        def _():
            part[slot, pl.ds(DK0, T), :] = jnp.zeros((T, HD), F32)
            part[slot, pl.ds(DV0, T), :] = jnp.zeros((T, HD), F32)

        cross_backward(pa, zb, slot)

        @pl.when(u == 0)
        def _():
            snd[0, 0, 1] = part[1].astype(BF16)
            rsz_start(1, 0, 1)
            rsz_start(1, 1, 1)
            on_plane(1, lambda: share(0).start())

        @pl.when(u == 1)
        def _():
            row_stage(hid, 1, 1)
            on_plane(0, lambda: share(0).wait_recv())
            snd[0, 0, 0] = (part[0] + xr[0].astype(F32)).astype(BF16)
            rsz_start(1, 0, 0)
            rsz_start(1, 1, 0)

        for hop in range(2, 5):

            @pl.when(v == 4 * (hop - 2) + 3)
            def _():
                for jj in (1, 0):

                    def pass_on(ww, inner):
                        rsz_wait(hop - 1, ww, jj)
                        terms = part[2 * ww + jj] + rcv[hop - 2, ww, jj].astype(F32)
                        if hop == 2 and jj == 0:
                            on_plane(0, lambda: share(1 + ww).wait_recv())
                            terms = terms + xr[1 + ww].astype(F32)
                        snd[hop - 1, ww, jj] = terms.astype(BF16)
                        rsz_start(hop, ww, jj)
                        return inner

                    lax.fori_loop(0, 2, pass_on, 0)
                row_stage(hid, 1, hop)

        return carry

    lax.fori_loop(0, NC - 1, backward_step, 0)
    self_backward(p, z, 1, True)
    cross_backward(p, z, 1)

    for j in range(1, NC):
        w_in(j).wait_recv()
    mix = jnp.zeros((T, HD), F32)
    for n in range(NC):
        mix = mix + nn(hid[n // 4, n % 2, (n // 2) % 2], wcol[n])
    mixed_ref[...] = mix.astype(BF16)
    gq_ref[...] = jnp.transpose(dq_t[...]) * SCALE
    gcq_ref[...] = jnp.transpose(dcq_t[...]) * SCALE

    rsz_wait(4, 0, 1)
    rsz_wait(4, 1, 1)
    xsnd[...] = (part[0] + rcv[3, 0, 1].astype(F32) + rcv[3, 1, 1].astype(F32)).astype(BF16)
    on_plane(0, lambda: rsx(True).start())
    on_plane(1, lambda: rsx(False).start())
    rsz_wait(4, 0, 0)
    rsz_wait(4, 1, 0)
    part[1] = part[1] + rcv[3, 0, 0].astype(F32) + rcv[3, 1, 0].astype(F32)
    on_plane(0, lambda: rsx(False).wait_recv())
    on_plane(1, lambda: rsx(True).wait_recv())

    def total(at, rows):
        return part[1, pl.ds(at, rows), :] + xrcv[pl.ds(at, rows), :].astype(F32)

    gk_ref[...] = total(DK0, T) * SCALE
    gv_ref[...] = total(DV0, T)
    grk_ref[...] = total(DRK0, TR) * SCALE
    grv_ref[...] = total(DRV0, TR)
    gw_ref[pl.ds(0, HD // 2), :] = total(GT0, HD // 2)
    gw_ref[pl.ds(HD // 2, HD // 2), :] = total(GB0, HD // 2)

    for plane in range(2):
        on_plane(plane, lambda: agx(True, plane).wait_send())
        on_plane(plane, lambda: rsx(plane == 0).wait_send())
    for n in range(3):
        on_plane(1, lambda: share(n).wait_send())
    for jj in range(2):
        for ww in range(2):
            for s in range(1, 5):
                agz_sent(s, ww, jj)
                rsz_sent(s, ww, jj)
    for n in range(9):
        row_copy(cot, 0, n, True).wait_send()
        row_copy(hid, 1, n, True).wait_send()
    for j in range(1, NC):
        w_out(j).wait_send()


def shards(queries, keys, values, cross_queries, row_keys, row_values, incidence, out_weight, cotangent):
    vmem = pl.BlockSpec(memory_space=pltpu.VMEM)
    hbm = pl.BlockSpec(memory_space=pl.ANY)
    dma = pltpu.SemaphoreType.DMA
    big, small = jax.ShapeDtypeStruct((T, HD), F32), jax.ShapeDtypeStruct((TR, HD), F32)
    wide = pltpu.VMEM((HD, T), F32)
    line = pltpu.VMEM((1, T), F32)
    return pl.pallas_call(
        body,
        out_shape=(jax.ShapeDtypeStruct((T, HD), BF16), big, big, big, big, small, small, small),
        in_specs=[vmem] * 4 + [hbm] * 5,
        out_specs=[vmem] * 8,
        scratch_shapes=[
            pltpu.VMEM((2, NZ, AG_ALL, HD), BF16),
            pltpu.VMEM((4, 2, 2, T, HD), BF16),
            pltpu.VMEM((4, 2, 2, T, HD), BF16),
            pltpu.VMEM((NC, HD, HD), BF16),
            pltpu.VMEM((4, 2, 2, RS_ALL, HD), BF16),
            pltpu.VMEM((4, 2, 2, RS_ALL, HD), BF16),
            pltpu.VMEM((4, RS_ALL, HD), F32),
            pltpu.VMEM((RS_ALL, HD), BF16),
            pltpu.VMEM((RS_ALL, HD), BF16),
            pltpu.VMEM((HD, T), BF16),
            pltpu.VMEM((HD, T), BF16),
            pltpu.VMEM((HD, T), BF16),
            pltpu.VMEM((T, HD), BF16),
            pltpu.VMEM((HD, T), BF16),
            wide, wide, line, line, line, line, line, line,
            pltpu.VMEM((NC, T), F32),
            wide, wide,
            pltpu.VMEM((3, RS_ALL, HD), BF16),
            dma((6,)), dma((1,)), dma((1,)), dma((4, 2, 2)), dma((4, 2, 2)), dma((4, 2, 2)), dma((4, 2, 2)),
            dma((1,)), dma((1,)), dma((2, 9)), dma((2, 9)), dma((NC,)), dma((NC,)),
            dma((4,)), dma((4,)), dma((3,)), dma((3,)),
        ],
        compiler_params=pltpu.CompilerParams(
            collective_id=0, has_side_effects=True, vmem_limit_bytes=60 * 1024 * 1024
        ),
        name="attention_layer",
    )(queries, cross_queries, incidence, out_weight, keys, values, row_keys, row_values, cotangent)


def solution(mesh):
    both = P("ctx", "row")
    return jax.shard_map(
        shards,
        mesh=mesh,
        in_specs=(both, both, both, both, both, both, P("ctx", None), P("row", None), both),
        out_specs=(both, both, both, both, both, both, both, P("row", "ctx")),
        check_vma=False,
    )
```

```python
import functools
import math

import jax
import jax.numpy as jnp
from jax import lax
from jax.experimental import pallas as pl
from jax.experimental.pallas import tpu as pltpu
from jax.sharding import PartitionSpec as P

MESH = pl.DeviceIdType.MESH
F32 = jnp.float32
BF16 = jnp.bfloat16
T = 512
HD = 128
TR = 128
NC = 16
NZ = 8
SCALE = 1.0 / math.sqrt(HD)
C2 = SCALE * math.log2(math.e)
LOG2E = math.log2(math.e)
NEG = -1e30

K0, RK0, RV0, V0, AG_HALF, AG_ALL = 0, 512, 640, 768, 640, 1280
AG_MID, AG_MID_N = 512, 256
DK0, DRK0, GT0, GB0, DRV0, DV0, RS_HALF, RS_ALL = 0, 512, 640, 704, 768, 896, 704, 1408
RS_MID, RS_MID_N = 512, 384


def nn(a, b):
    return lax.dot_general(a, b, (((1,), (0,)), ((), ())), preferred_element_type=F32)


def nt(a, b):
    return lax.dot_general(a, b, (((1,), (1,)), ((), ())), preferred_element_type=F32)


def tn(a, b):
    return lax.dot_general(a, b, (((0,), (0,)), ((), ())), preferred_element_type=F32)


def body(
    q_ref, cq_ref, inc_ref, w_ref, k_hbm, v_hbm, rk_hbm, rv_hbm, cot_hbm,
    mixed_ref, gq_ref, gk_ref, gv_ref, gcq_ref, grk_ref, grv_ref, gw_ref,
    kv, cot, hid, wcol, snd, rcv, part, xsnd, xrcv, qt, cqt, dot_t, do_ref, ht,
    acc_s, acc_c, m_s, l_s, m_c, l_c, dl_s, dl_c, bias, dq_t, dcq_t, xr,
    lsem, agx_s, agx_r, agz_s, agz_r, rsz_s, rsz_r, rsx_s, rsx_r, row_s, row_r, w_s, w_r,
    rel_s, rel_r, shr_s, shr_r,
):
    c = lax.axis_index("ctx")
    r = lax.axis_index("row")
    p, z = c // NZ, c % NZ
    y, xh, core = r // 4, (r // 2) % 2, r % 2

    def ctx_at(plane, depth):
        return {"ctx": plane * NZ + (depth + NZ) % NZ}

    def row_at(yy, xx, cc):
        return {"row": (((yy + 4) % 4) * 2 + xx) * 2 + cc}

    def plane_of(j):
        return p + j * (1 - 2 * p)

    def zmod(d):
        return (z + d + NZ) % NZ

    def remote(src, dst, ssem, rsem, device):
        return pltpu.make_async_remote_copy(
            src_ref=src, dst_ref=dst, send_sem=ssem, recv_sem=rsem, device_id=device, device_id_type=MESH
        )

    def on_plane(plane, act):
        pl.when(p == plane)(act)

    def agx(out, plane):
        ref = kv.at[p if out else 1 - p, z]
        if (plane == 1) == out:
            ref = ref.at[pl.ds(AG_MID, AG_MID_N)]
        return remote(ref, ref, agx_s.at[0], agx_r.at[0], ctx_at(1 - p, z))

    def agz(s, way, j, out, middle):
        ref = kv.at[plane_of(j), zmod((2 * way - 1) * (s - 1 if out else s))]
        half = s == 4
        if middle:
            n = AG_MID_N // 2 if half else AG_MID_N
            ref = ref.at[pl.ds(AG_MID + (way * n if half else 0), n)]
        elif half:
            ref = ref.at[pl.ds(way * AG_HALF, AG_HALF)]
        return remote(ref, ref, agz_s.at[s - 1, way, j], agz_r.at[s - 1, way, j], ctx_at(p, z + 1 - 2 * way))

    def relay(s, way):
        ref = kv.at[0, zmod((2 * way - 1) * s)]
        if s == 4:
            ref = ref.at[pl.ds(way * AG_HALF, AG_HALF)]
        n = 2 * (s - 3) + way
        return remote(ref, ref, rel_s.at[n], rel_r.at[n], ctx_at(1 - p, z))

    def agz_start(s, way, j):
        if j == 0:
            agz(s, way, 0, True, False).start()
            return
        on_plane(0, lambda: agz(s, way, 1, True, True).start())
        if s < 3:
            on_plane(1, lambda: agz(s, way, 1, True, False).start())

    def agz_wait(s, way, j):
        if j == 0:
            agz(s, way, 0, False, False).wait_recv()
            if s >= 3:
                on_plane(0, lambda: relay(s, way).start())
            return
        on_plane(0, lambda: agz(s, way, 1, False, True).wait_recv())
        on_plane(1, lambda: (agz(s, way, 1, False, False) if s < 3 else relay(s, way)).wait_recv())

    def agz_sent(s, way, j):
        if j == 0:
            agz(s, way, 0, True, False).wait_send()
            if s >= 3:
                on_plane(0, lambda: relay(s, way).wait_send())
            return
        on_plane(0, lambda: agz(s, way, 1, True, True).wait_send())
        if s < 3:
            on_plane(1, lambda: agz(s, way, 1, True, False).wait_send())

    def rsz(s, way, j, middle):
        half = s == 1
        src = snd.at[0, 0, j] if half else snd.at[s - 1, way, j]
        dst = rcv.at[s - 1, way, j]
        if middle:
            n = RS_MID_N // 2 if half else RS_MID_N
            rows = pl.ds(RS_MID + (way * n if half else 0), n)
            src, dst = src.at[rows], dst.at[rows]
        elif half:
            rows = pl.ds(way * RS_HALF, RS_HALF)
            src, dst = src.at[rows], dst.at[rows]
        return remote(src, dst, rsz_s.at[s - 1, way, j], rsz_r.at[s - 1, way, j], ctx_at(p, z + 1 - 2 * way))

    def share(n):
        src = snd.at[0, 0, 1] if isinstance(n, int) and n == 0 else snd.at[1, n - 1, 1]
        return remote(src, xr.at[n], shr_s.at[n], shr_r.at[n], ctx_at(1 - p, z))

    def rsz_start(s, way, j):
        if j == 0:
            rsz(s, way, 0, False).start()
            return
        on_plane(0, lambda: rsz(s, way, 1, True).start())
        if s >= 3:
            on_plane(1, lambda: rsz(s, way, 1, False).start())
        elif s == 2:
            on_plane(1, lambda: share(1 + way).start())

    def rsz_wait(s, way, j):
        if j == 0:
            rsz(s, way, 0, False).wait_recv()
            return
        on_plane(0, lambda: rsz(s, way, 1, True).wait_recv())
        if s >= 3:
            on_plane(1, lambda: rsz(s, way, 1, False).wait_recv())

    def rsz_sent(s, way, j):
        if j == 0:
            rsz(s, way, 0, False).wait_send()
            return
        on_plane(0, lambda: rsz(s, way, 1, True).wait_send())
        if s >= 3:
            on_plane(1, lambda: rsz(s, way, 1, False).wait_send())

    def rsx(middle):
        rows = pl.ds(RS_MID, RS_MID_N) if middle else pl.ds(0, RS_ALL)
        return remote(xsnd.at[rows], xrcv.at[rows], rsx_s.at[0], rsx_r.at[0], ctx_at(1 - p, z))

    def row_copy(buf, k, n, out):
        up, down, sib = row_at(y + 1, xh, core), row_at(y - 1, xh, core), row_at(y, xh, 1 - core)
        ym, yp, y2 = (y + 3) % 4, (y + 1) % 4, (y + 2) % 4
        mine, other = (core, core) if n < 5 else (core, 1 - core)
        if n == 0:
            ref = buf.at[y, core, xh if out else 1 - xh]
            dev = row_at(y, 1 - xh, core)
        elif n == 1:
            ref, dev = buf.at[y if out else ym, core], up
        elif n == 2:
            ref, dev = buf.at[y if out else yp, core], down
        elif n == 3:
            ref, dev = buf.at[ym if out else y2, core, :, pl.ds(0, T // 2)], up
        elif n == 4:
            ref, dev = buf.at[yp if out else y2, core, :, pl.ds(T // 2, T // 2)], down
        else:
            at = (y, ym, yp, y2)[n - 5]
            ref, dev = buf.at[at, mine if out else other], sib
        return remote(ref, ref, row_s.at[k, n], row_r.at[k, n], dev)

    def row_stage(buf, k, stage):
        waits, starts = {
            0: ((), (0,)), 1: ((0,), (1, 2, 5)), 2: ((1, 2), (3, 4, 6, 7)), 3: ((3, 4), (8,)), 4: ((5, 6, 7, 8), ()),
        }[stage]
        for n in waits:
            row_copy(buf, k, n, False).wait_recv()
        for n in starts:
            row_copy(buf, k, n, True).start()

    def w_out(j):
        to = (r + j) % NC
        return remote(
            w_ref.at[:, pl.ds(pl.multiple_of(to * HD, HD), HD)], wcol.at[r], w_s.at[j], w_r.at[j], {"row": to}
        )

    def w_in(j):
        at = (r + NC - j) % NC
        return remote(wcol.at[at], wcol.at[at], w_s.at[j], w_r.at[j], {"row": at})

    own = kv.at[p, z]
    loads = [
        pltpu.make_async_copy(k_hbm, own.at[pl.ds(K0, T)], lsem.at[0]),
        pltpu.make_async_copy(rk_hbm, own.at[pl.ds(RK0, TR)], lsem.at[1]),
        pltpu.make_async_copy(v_hbm, own.at[pl.ds(V0, T)], lsem.at[2]),
        pltpu.make_async_copy(rv_hbm, own.at[pl.ds(RV0, TR)], lsem.at[3]),
        pltpu.make_async_copy(cot_hbm, cot.at[y, core, xh], lsem.at[4]),
        pltpu.make_async_copy(w_ref.at[:, pl.ds(pl.multiple_of(r * HD, HD), HD)], wcol.at[r], lsem.at[5]),
    ]
    for load in loads:
        load.start()
    barrier = pltpu.get_barrier_semaphore()
    for device in (ctx_at(1 - p, z), ctx_at(p, z + 1), ctx_at(p, z - 1)):
        pl.semaphore_signal(barrier, inc=1, device_id=device, device_id_type=MESH)

    def greet(j, carry):
        pl.semaphore_signal(barrier, inc=1, device_id={"row": (r + j) % NC}, device_id_type=MESH)
        return carry

    lax.fori_loop(1, NC, greet, 0)
    for load in loads:
        load.wait()
    pl.semaphore_wait(barrier, NC + 2)

    for plane in range(2):
        on_plane(plane, lambda: agx(True, plane).start())
    agz_start(1, 0, 0)
    agz_start(1, 1, 0)
    row_stage(cot, 0, 0)

    qt[...] = jnp.transpose(q_ref[...].astype(F32)).astype(BF16)
    cqt[...] = jnp.transpose(cq_ref[...].astype(F32)).astype(BF16)
    lanes = lax.broadcasted_iota(jnp.int32, (T, HD), 1)
    hit = jnp.zeros((T, HD), F32)
    for n in range(4):
        hit = jnp.where(inc_ref[:, n : n + 1] == lanes, 1.0, hit)
    bias[...] = (jnp.transpose(hit)[0:NC, :] - 1.0) * (-NEG)
    for ref in (acc_s, acc_c, l_s, l_c, dq_t, dcq_t):
        ref[...] = jnp.zeros_like(ref)
    for ref in (m_s, m_c):
        ref[...] = jnp.full_like(ref, NEG)
    for j in range(2):
        rcv[0, 0, j, RS_HALF:, :] = jnp.zeros((RS_ALL - RS_HALF, HD), BF16)
        rcv[0, 1, j, :RS_HALF, :] = jnp.zeros((RS_HALF, HD), BF16)

    @pl.when(p == 1)
    def _():
        for way in range(2):
            rcv[0, way, 1] = jnp.zeros((RS_ALL, HD), BF16)
            rcv[1, way, 1] = jnp.zeros((RS_ALL, HD), BF16)
        xr[...] = jnp.zeros_like(xr)
        xrcv[...] = jnp.zeros_like(xrcv)

    def online(logits, values, m_ref, l_ref, acc_ref):
        m_old = m_ref[...]
        m_new = jnp.maximum(m_old, jnp.max(logits, axis=0, keepdims=True))
        probs = jnp.exp2(logits - m_new)
        fade = jnp.exp2(m_old - m_new)
        l_ref[...] = l_ref[...] * fade + jnp.sum(probs, axis=0, keepdims=True)
        acc_ref[...] = acc_ref[...] * fade + tn(values, probs.astype(BF16))
        m_ref[...] = m_new

    def causal(x, fill):
        keep = lax.broadcasted_iota(jnp.int32, (T, T), 0) <= lax.broadcasted_iota(jnp.int32, (T, T), 1)
        return jnp.where(keep, x, fill)

    def self_forward(pa, zb, diagonal):
        logits = nn(kv[pa, zb, pl.ds(K0, T), :], qt[...]) * C2
        if diagonal:
            logits = causal(logits, NEG)
        online(logits, kv[pa, zb, pl.ds(V0, T), :], m_s, l_s, acc_s)

    def cross_logits(pa, zb):
        return nn(kv[pa, zb, pl.ds(RK0, TR), :], cqt[...]) * C2 + bias[pl.ds(pa * NZ + zb, 1), :]

    def cross_forward(pa, zb):
        online(cross_logits(pa, zb), kv[pa, zb, pl.ds(RV0, TR), :], m_c, l_c, acc_c)

    self_forward(p, z, True)
    cross_forward(p, z)

    def hidden_grad():
        grad = jnp.zeros((T, HD), F32)
        for n in range(NC):
            grad = grad + nt(cot[n // 4, n % 2, (n // 2) % 2], w_ref[:, n * HD : (n + 1) * HD])
        grad = grad.astype(BF16)
        do_ref[...] = grad
        dot_t[...] = jnp.transpose(grad.astype(F32)).astype(BF16)

    def forward_step(t, carry):
        v = t - 2
        s = jnp.where(t < 2, 0, v // 4 + 1)
        i = jnp.where(t < 2, 1, v % 4)
        way, j = jnp.where(s == 3, i % 2, i // 2), jnp.where(s == 3, i // 2, i % 2)

        @pl.when(t == 1)
        def _():
            for plane in range(2):
                on_plane(plane, lambda: agx(False, plane).wait_recv())
            agz_start(1, 0, 1)
            agz_start(1, 1, 1)
            row_stage(cot, 0, 1)

        def arrive(hop, jj):
            for ww in range(2):
                agz_wait(hop, ww, jj)
                if hop < 4:
                    agz_start(hop + 1, ww, jj)

        for hop in range(1, 5):

            @pl.when(v == 4 * (hop - 1))
            def _():
                arrive(hop, 0)
                if hop < 3:
                    arrive(hop, 1)
                if hop == 1:
                    for jj in range(1, NC):
                        w_out(jj).start()
                if hop < 4:
                    row_stage(cot, 0, hop + 1)
                if hop == 3:
                    hidden_grad()

            if hop > 2:

                @pl.when(v == (10 if hop == 3 else 13))
                def _():
                    arrive(hop, 1)

        pa = plane_of(j)
        zb = zmod((2 * way - 1) * s)

        @pl.when(pa * NZ + zb < c)
        def _():
            self_forward(pa, zb, False)

        cross_forward(pa, zb)
        return carry

    lax.fori_loop(1, NC, forward_step, 0)

    grad_t = dot_t[...].astype(F32)
    out_s = acc_s[...] / l_s[...]
    out_c = acc_c[...] / l_c[...]
    hidden_t = out_s + out_c
    ht[...] = hidden_t.astype(BF16)
    hid[y, core, xh] = jnp.transpose(hidden_t).astype(BF16)
    dl_s[...] = jnp.sum(grad_t * out_s, axis=0, keepdims=True)
    dl_c[...] = jnp.sum(grad_t * out_c, axis=0, keepdims=True)
    m_s[...] = m_s[...] + jnp.log(l_s[...]) * LOG2E
    m_c[...] = m_c[...] + jnp.log(l_c[...]) * LOG2E
    row_stage(hid, 1, 0)

    def logit_grads(logits, lse_ref, delta_ref, values, diagonal):
        probs = jnp.exp2(logits - lse_ref[...])
        if diagonal:
            probs = causal(probs, 0.0)
        dlogits = probs * (nn(values, dot_t[...]) - delta_ref[...])
        return probs.astype(BF16), dlogits.astype(BF16)

    def self_backward(pa, zb, slot, diagonal):
        keys, values = kv[pa, zb, pl.ds(K0, T), :], kv[pa, zb, pl.ds(V0, T), :]
        probs, dlogits = logit_grads(nn(keys, qt[...]) * C2, m_s, dl_s, values, diagonal)
        part[slot, pl.ds(DV0, T), :] = nn(probs, do_ref[...])
        part[slot, pl.ds(DK0, T), :] = nn(dlogits, q_ref[...])
        dq_t[...] += tn(keys, dlogits)

    def cross_backward(pa, zb, slot):
        probs, dlogits = logit_grads(cross_logits(pa, zb), m_c, dl_c, kv[pa, zb, pl.ds(RV0, TR), :], False)
        part[slot, pl.ds(DRV0, TR), :] = nn(probs, do_ref[...])
        part[slot, pl.ds(DRK0, TR), :] = nn(dlogits, cq_ref[...])
        dcq_t[...] += tn(kv[pa, zb, pl.ds(RK0, TR), :], dlogits)
        b = pa * NZ + zb
        weight = nn(ht[...], cot[b // 4, b % 2, (b // 2) % 2])
        part[slot, pl.ds(GT0, HD // 2), :] = weight[: HD // 2]
        part[slot, pl.ds(GB0, HD // 2), :] = weight[HD // 2 :]

    def backward_step(u, carry):
        v = u - 2
        first, last = u < 2, u == 14
        s = jnp.where(first, 1, v // 4 + 2)
        i = v % 4
        way = jnp.where(first | last, 0, i % 2)
        j = jnp.where(first, 1 - u, jnp.where(last, 1, 1 - i // 2))
        slot = jnp.where(last, 0, 2 * way + j)
        d = 5 - s
        pa = plane_of(j)
        zb = zmod((1 - 2 * way) * d)

        @pl.when(pa * NZ + zb < c)
        def _():
            self_backward(pa, zb, slot, False)

        @pl.when(pa * NZ + zb > c)
        def _():
            part[slot, pl.ds(DK0, T), :] = jnp.zeros((T, HD), F32)
            part[slot, pl.ds(DV0, T), :] = jnp.zeros((T, HD), F32)

        cross_backward(pa, zb, slot)

        @pl.when(u == 0)
        def _():
            snd[0, 0, 1] = part[1].astype(BF16)
            rsz_start(1, 0, 1)
            rsz_start(1, 1, 1)
            on_plane(1, lambda: share(0).start())

        @pl.when(u == 1)
        def _():
            row_stage(hid, 1, 1)
            on_plane(0, lambda: share(0).wait_recv())
            snd[0, 0, 0] = (part[0] + xr[0].astype(F32)).astype(BF16)
            rsz_start(1, 0, 0)
            rsz_start(1, 1, 0)

        def pass_on(hop, jj):
            def one(ww, inner):
                rsz_wait(hop - 1, ww, jj)
                terms = part[2 * ww + jj] + rcv[hop - 2, ww, jj].astype(F32)
                if hop == 2 and jj == 0:
                    on_plane(0, lambda: share(1 + ww).wait_recv())
                    terms = terms + xr[1 + ww].astype(F32)
                snd[hop - 1, ww, jj] = terms.astype(BF16)
                rsz_start(hop, ww, jj)
                return inner

            lax.fori_loop(0, 2, one, 0)

        for hop in range(2, 5):

            @pl.when(v == 4 * (hop - 2) + 1)
            def _():
                pass_on(hop, 1)

            @pl.when(v == 4 * (hop - 2) + 3)
            def _():
                pass_on(hop, 0)
                row_stage(hid, 1, hop)

        return carry

    lax.fori_loop(0, NC - 1, backward_step, 0)
    self_backward(p, z, 1, True)
    cross_backward(p, z, 1)

    for j in range(1, NC):
        w_in(j).wait_recv()
    mix = jnp.zeros((T, HD), F32)
    for n in range(NC):
        mix = mix + nn(hid[n // 4, n % 2, (n // 2) % 2], wcol[n])
    mixed_ref[...] = mix.astype(BF16)
    gq_ref[...] = jnp.transpose(dq_t[...]) * SCALE
    gcq_ref[...] = jnp.transpose(dcq_t[...]) * SCALE

    rsz_wait(4, 0, 1)
    rsz_wait(4, 1, 1)
    xsnd[...] = (part[0] + rcv[3, 0, 1].astype(F32) + rcv[3, 1, 1].astype(F32)).astype(BF16)
    on_plane(0, lambda: rsx(True).start())
    on_plane(1, lambda: rsx(False).start())
    rsz_wait(4, 0, 0)
    rsz_wait(4, 1, 0)
    part[1] = part[1] + rcv[3, 0, 0].astype(F32) + rcv[3, 1, 0].astype(F32)
    on_plane(0, lambda: rsx(False).wait_recv())
    on_plane(1, lambda: rsx(True).wait_recv())

    def total(at, rows):
        return part[1, pl.ds(at, rows), :] + xrcv[pl.ds(at, rows), :].astype(F32)

    gk_ref[...] = total(DK0, T) * SCALE
    gv_ref[...] = total(DV0, T)
    grk_ref[...] = total(DRK0, TR) * SCALE
    grv_ref[...] = total(DRV0, TR)
    gw_ref[pl.ds(0, HD // 2), :] = total(GT0, HD // 2)
    gw_ref[pl.ds(HD // 2, HD // 2), :] = total(GB0, HD // 2)

    for plane in range(2):
        on_plane(plane, lambda: agx(True, plane).wait_send())
        on_plane(plane, lambda: rsx(plane == 0).wait_send())
    for n in range(3):
        on_plane(1, lambda: share(n).wait_send())
    for jj in range(2):
        for ww in range(2):
            for s in range(1, 5):
                agz_sent(s, ww, jj)
                rsz_sent(s, ww, jj)
    for n in range(9):
        row_copy(cot, 0, n, True).wait_send()
        row_copy(hid, 1, n, True).wait_send()
    for j in range(1, NC):
        w_out(j).wait_send()


def shards(queries, keys, values, cross_queries, row_keys, row_values, incidence, out_weight, cotangent):
    vmem = pl.BlockSpec(memory_space=pltpu.VMEM)
    hbm = pl.BlockSpec(memory_space=pl.ANY)
    dma = pltpu.SemaphoreType.DMA
    big, small = jax.ShapeDtypeStruct((T, HD), F32), jax.ShapeDtypeStruct((TR, HD), F32)
    wide = pltpu.VMEM((HD, T), F32)
    line = pltpu.VMEM((1, T), F32)
    return pl.pallas_call(
        body,
        out_shape=(jax.ShapeDtypeStruct((T, HD), BF16), big, big, big, big, small, small, small),
        in_specs=[vmem] * 4 + [hbm] * 5,
        out_specs=[vmem] * 8,
        scratch_shapes=[
            pltpu.VMEM((2, NZ, AG_ALL, HD), BF16),
            pltpu.VMEM((4, 2, 2, T, HD), BF16),
            pltpu.VMEM((4, 2, 2, T, HD), BF16),
            pltpu.VMEM((NC, HD, HD), BF16),
            pltpu.VMEM((4, 2, 2, RS_ALL, HD), BF16),
            pltpu.VMEM((4, 2, 2, RS_ALL, HD), BF16),
            pltpu.VMEM((4, RS_ALL, HD), F32),
            pltpu.VMEM((RS_ALL, HD), BF16),
            pltpu.VMEM((RS_ALL, HD), BF16),
            pltpu.VMEM((HD, T), BF16),
            pltpu.VMEM((HD, T), BF16),
            pltpu.VMEM((HD, T), BF16),
            pltpu.VMEM((T, HD), BF16),
            pltpu.VMEM((HD, T), BF16),
            wide, wide, line, line, line, line, line, line,
            pltpu.VMEM((NC, T), F32),
            wide, wide,
            pltpu.VMEM((3, RS_ALL, HD), BF16),
            dma((6,)), dma((1,)), dma((1,)), dma((4, 2, 2)), dma((4, 2, 2)), dma((4, 2, 2)), dma((4, 2, 2)),
            dma((1,)), dma((1,)), dma((2, 9)), dma((2, 9)), dma((NC,)), dma((NC,)),
            dma((4,)), dma((4,)), dma((3,)), dma((3,)),
        ],
        compiler_params=pltpu.CompilerParams(
            collective_id=0, has_side_effects=True, vmem_limit_bytes=60 * 1024 * 1024
        ),
        name="attention_layer",
    )(queries, cross_queries, incidence, out_weight, keys, values, row_keys, row_values, cotangent)


def solution(mesh):
    both = P("ctx", "row")
    return jax.shard_map(
        shards,
        mesh=mesh,
        in_specs=(both, both, both, both, both, both, P("ctx", None), P("row", None), both),
        out_specs=(both, both, both, both, both, both, both, P("row", "ctx")),
        check_vma=False,
    )
```
